32 devices in a mesh: groups: 2 (over y), row: 8 (over z, x), col: 2 (over core).
Axes of the slice: x: 2, y: 2, z: 4, core: 2. Of those that a mesh axis runs over, the one named last changes fastest.
Arguments:
- tokens: bfloat16 [1024, 6144], P(('groups', 'row'), 'col'), parts along dimension 0, may hold values from -6 to 6
- w_qkv: bfloat16 [6144, 12288], P('col', 'row'), may hold values from -0.078125 to 0.078125
- query_gain: float32 [128], replicated, may hold values from 0.5 to 1.5
- key_gain: float32 [128], replicated, may hold values from 0.5 to 1.5
- logit_scale: float32 [32], replicated, may hold values from 1 to 3
Outputs:
- attended: bfloat16 [1024, 4096], P(('groups', 'row', 'col')), parts along dimension 0
The draws below stay inside these ranges and needn't reach their ends.
There are 2 independent parts, one for each index of `groups`. The reference program is written for one: setup_inputs(seed, part) draws one part's arguments, and reference() takes and returns one part's arrays. A program takes and returns all parts, laid end to end along the dimension named above; an argument that names none is the same for every part. Nothing has to cross between parts.
All inputs are finite; a program needn't handle non-finite values.
Results may differ from the reference program's by a relative error of at most 0.0091.
Values may be sent and summed in bfloat16 or wider, within the bound.
A program may use at most 128 MiB of HBM per device.

```python
import math
import jax
import jax.numpy as jnp
from jax import lax

D = 6144
H = 32
K = 128
TOKENS = 512


def level_of(key, extent, split, smallest, largest):
    level = 1.0
    for dim, shards_of in split:
        heights = jax.random.uniform(jax.random.fold_in(jax.random.fold_in(key, 6), dim), (shards_of,), jnp.float32, smallest / len(split), largest / len(split))
        level = level * jnp.repeat(jnp.exp(heights), extent[dim] // shards_of).reshape((-1,) + (1,) * (len(extent) - 1 - dim))
    return level


def normal_values(rng, extent, width, bound, pieces=(), kind=jnp.bfloat16):
    loudness = level_of(rng, extent, pieces, -0.22, 0.18) if pieces else 1.0
    entries = jax.random.normal(rng, extent, jnp.float32) * width * loudness
    return jnp.minimum(jnp.maximum(entries, -bound), bound).astype(kind)


def setup_inputs(seed: int = 0, part: int = 0) -> dict:
    keys = jax.random.split(jax.random.key(seed), 6)
    part_splits = jax.random.split(jax.random.fold_in(keys[5], part), 6)
    tokens = normal_values(part_splits[0], (TOKENS, D), 1.0, 6.0, ((0, 8), (1, 2)))
    w_qkv = normal_values(keys[1], (D, 3 * H * K), D ** -0.5, 0.078125, ((0, 2), (1, 8)))
    query_gain = jnp.clip(1.0 + 0.1 * jax.random.normal(keys[2], (K,), jnp.float32), 0.5, 1.5)
    key_gain = jnp.clip(1.0 + 0.1 * jax.random.normal(keys[3], (K,), jnp.float32), 0.5, 1.5)
    logit_scale = jnp.clip(jnp.exp(jax.random.uniform(keys[4], (H,), jnp.float32, math.log(1.0), math.log(3.0))), 1.0, 3.0)
    return dict(tokens=tokens, w_qkv=w_qkv, query_gain=query_gain, key_gain=key_gain, logit_scale=logit_scale)


def rms_scale(values, gain):
    wide = values.astype(jnp.float32)
    power = lax.optimization_barrier(jnp.mean(wide * wide, axis=-1, keepdims=True))
    return (wide * lax.rsqrt(power + 1e-06) * gain).astype(jnp.bfloat16)

def reference(tokens, w_qkv, query_gain, key_gain, logit_scale):
    qkv = jnp.dot(tokens, w_qkv, preferred_element_type=jnp.float32).astype(jnp.bfloat16)
    halves = qkv.reshape(TOKENS, 2, H, 3, K // 2)
    joined = jnp.concatenate([halves[:, 0], halves[:, 1]], axis=-1)
    query_normed = rms_scale(joined[:, :, 0], query_gain)
    key_normed = rms_scale(joined[:, :, 1], key_gain)
    value = joined[:, :, 2]
    inv_root = 1.0 / math.sqrt(K)

    def one_head(packed):
        q_head, k_head, v_head, scale = packed
        scores = jnp.dot(q_head, k_head.T, preferred_element_type=jnp.float32) * (scale * inv_root)
        expo = jnp.exp(scores)
        probs = (expo / lax.optimization_barrier(jnp.sum(expo, axis=-1, keepdims=True))).astype(jnp.bfloat16)
        return jnp.dot(probs, v_head, preferred_element_type=jnp.float32).astype(jnp.bfloat16)
    outputs = lax.map(one_head, (jnp.swapaxes(query_normed, 0, 1), jnp.swapaxes(key_normed, 0, 1), jnp.swapaxes(value, 0, 1), logit_scale))
    return jnp.swapaxes(outputs, 0, 1).reshape(TOKENS, H * K)
```

```python
import functools
import math

import jax
import jax.numpy as jnp
from jax import lax
from jax.experimental import pallas as pl
from jax.experimental.pallas import tpu as pltpu
from jax.sharding import PartitionSpec as P

MESH = pl.DeviceIdType.MESH
FAST = 2
TILE = 256


def visit_order(depth):
    return [sorted(range(depth), key=lambda other: (abs(other - z), other)) for z in range(depth)]


def pick(index, values):
    chosen = jnp.int32(values[0])
    for i, value in enumerate(values[1:], 1):
        chosen = jnp.where(index == i, jnp.int32(value), chosen)
    return chosen


def fused_kernel(
    row_count, local_heads, head_dim,
    tokens, w_qkv, query_gain, key_gain, logit_scale, out,
    toks, weights, part_out, part_in, acc, joined, crossing, qn, kn, vv, att,
    own_sem, w_sem, gather_send, gather_recv, part_send, part_recv,
    cross_send, cross_recv, out_send, out_recv, self_sem,
):
    depth = row_count // FAST
    half_rows = row_count // 2
    half_dim = head_dim // 2
    heads = local_heads // 4
    span = heads * 3 * half_dim
    tok_rows = tokens.shape[0]
    slab = FAST * tok_rows
    out_rows = tok_rows // 2
    order = visit_order(depth)

    row = lax.axis_index("row")
    col = lax.axis_index("col")
    z = row // FAST
    x = lax.rem(row, FAST)
    side = row // half_rows
    group = lax.rem(row, half_rows)
    other_col = 1 - col
    other_row = lax.rem(row + half_rows, row_count)
    across = z * FAST + (1 - x)
    me = row * 2 + col

    def w_copy(dest_col, far):
        dest_side = side if far == 0 else 1 - side
        mine = 0 if dest_col is other_col else 1
        start = pl.multiple_of((dest_side * 2 + dest_col) * span, 128)
        return pltpu.make_async_copy(
            w_qkv.at[:, pl.ds(start, span)],
            weights.at[:, pl.ds((mine * 2 + far) * span, span)],
            w_sem.at[mine * 2 + far],
        )

    w_copies = [w_copy(c, far) for c in (other_col, col) for far in (0, 1)]
    own_copy = pltpu.make_async_copy(
        tokens, toks.at[pl.ds(pl.multiple_of(row * tok_rows, tok_rows), tok_rows)], own_sem
    )
    own_copy.start()

    barrier = pltpu.get_barrier_semaphore()
    for step in range(row_count):
        for c in (0, 1):
            if step == 0 and c == 0:
                continue
            peer = lax.rem(row + step, row_count)
            pl.semaphore_signal(
                barrier, inc=1,
                device_id={"row": peer, "col": col if c == 0 else other_col},
                device_id_type=MESH,
            )
    pl.semaphore_wait(barrier, 2 * row_count - 1)

    def block_at(block):
        return toks.at[pl.ds(pl.multiple_of(block * tok_rows, tok_rows), tok_rows)]

    def gather_copy(block, way, target, source=None):
        return pltpu.make_async_remote_copy(
            src_ref=block_at(block) if source is None else source,
            dst_ref=block_at(block),
            send_sem=gather_send.at[way, block],
            recv_sem=gather_recv.at[block],
            device_id={"row": target},
            device_id_type=MESH,
        )

    def column(distance, act):
        for sign in (0,) if distance == 0 else (-1, 1):
            at = z + sign * distance
            block = at * FAST + x
            source = tokens if distance == 0 else None

            @pl.when(jnp.logical_and(at >= 0, at < depth))
            def _():
                if act == "start" and distance:
                    gather_copy(block, 0, across).wait_recv()

                def go(copy):
                    if act == "start":
                        copy.start()
                    else:
                        copy.wait_send()

                if sign <= 0:

                    @pl.when(z + 1 < depth)
                    def _():
                        go(gather_copy(block, 1, row + FAST, source))

                if sign >= 0:

                    @pl.when(z >= 1)
                    def _():
                        go(gather_copy(block, 2, row - FAST, source))

                go(gather_copy(block, 0, across, source))

    def part_copy(k):
        return pltpu.make_async_remote_copy(
            src_ref=part_out.at[k], dst_ref=part_in.at[k],
            send_sem=part_send.at[k], recv_sem=part_recv.at[k],
            device_id={"col": other_col}, device_id_type=MESH,
        )

    def slab_of(at):
        return pl.ds(pl.multiple_of(at * slab, slab), slab)

    def cross_copy(k, at):
        return pltpu.make_async_remote_copy(
            src_ref=crossing.at[k], dst_ref=joined.at[side, slab_of(at)],
            send_sem=cross_send.at[k], recv_sem=cross_recv.at[at],
            device_id={"row": other_row}, device_id_type=MESH,
        )

    def batch(k):
        at = pick(z, [seq[k] for seq in order])
        gather_copy(at * FAST + (1 - x), 0, across).wait_recv()
        if k == 0:
            own_copy.wait()
            for copy in w_copies:
                copy.wait()
        rows = slab_of(at)
        tiles = 2 * span // TILE

        @pl.loop(0, tiles)
        def _(n):
            part_out[k, :, pl.ds(pl.multiple_of(n * TILE, TILE), TILE)] = jnp.dot(
                toks[rows, :], weights[:, pl.ds(pl.multiple_of(n * TILE, TILE), TILE)],
                preferred_element_type=jnp.float32,
            )

        part_copy(k).start()

        @pl.loop(0, tiles)
        def _(n):
            acc[:, pl.ds(pl.multiple_of(n * TILE, TILE), TILE)] = jnp.dot(
                toks[rows, :], weights[:, pl.ds(pl.multiple_of(2 * span + n * TILE, TILE), TILE)],
                preferred_element_type=jnp.float32,
            )

        part_copy(k).wait_recv()
        crossing[k] = (acc[:, span:] + part_in[k, :, span:]).astype(jnp.bfloat16)
        cross_copy(k, at).start()
        joined[side, rows, :] = (acc[:, :span] + part_in[k, :, :span]).astype(jnp.bfloat16)

    column(0, "start")
    for copy in w_copies:
        copy.start()
    column(1, "start")
    for k in range(depth):
        batch(k)
        if k + 2 < depth:
            column(k + 2, "start")

    lanes = lax.broadcasted_iota(jnp.int32, (slab, head_dim), 1)
    low = lanes < half_dim

    def prepare(at):
        pltpu.make_async_remote_copy(
            src_ref=crossing.at[0], dst_ref=joined.at[1 - side, slab_of(at)],
            send_sem=cross_send.at[0], recv_sem=cross_recv.at[at],
            device_id={"row": other_row}, device_id_type=MESH,
        ).wait_recv()
        rows = slab_of(at)

        def pair(piece):
            first = joined[0, rows, piece * head_dim:(piece + 1) * head_dim].astype(jnp.float32)
            second = joined[1, rows, piece * head_dim:(piece + 1) * head_dim].astype(jnp.float32)
            return (
                jnp.where(low, first, pltpu.roll(second, half_dim, 1)),
                jnp.where(low, pltpu.roll(first, half_dim, 1), second),
            )

        def normed(wide, gain):
            power = jnp.mean(wide * wide, axis=-1, keepdims=True)
            return (wide * lax.rsqrt(power + 1e-06) * gain[...]).astype(jnp.bfloat16)

        for j in range(heads // 2):
            parts = [part for piece in range(3) for part in pair(3 * j + piece)]
            for i in range(2):
                query, key, value = parts[3 * i:3 * i + 3]
                qn[2 * j + i, rows, :] = normed(query, query_gain)
                kn[2 * j + i, rows, :] = normed(key, key_gain)
                vv[2 * j + i, rows, :] = value.astype(jnp.bfloat16)

    for k in range(depth):
        prepare(pick(z, [seq[k] for seq in order]))

    first_head = group * local_heads + (side * 2 + col) * heads
    out_cols = pl.ds(pl.multiple_of(first_head * head_dim, heads * head_dim), heads * head_dim)
    inv_root = 1.0 / math.sqrt(head_dim)

    def out_copies(at, act):
        for xx in range(FAST):
            for cc in (0, 1):
                target = at * FAST + xx
                source = att.at[
                    pl.ds(pl.multiple_of(target * tok_rows + cc * out_rows, out_rows), out_rows)
                ]
                is_me = jnp.logical_and(target == row, col == cc)

                @pl.when(is_me)
                def _():
                    copy = pltpu.make_async_copy(source, out.at[:, out_cols], self_sem)
                    copy.start() if act == "start" else copy.wait()

                @pl.when(jnp.logical_not(is_me))
                def _():
                    copy = pltpu.make_async_remote_copy(
                        src_ref=source, dst_ref=out.at[:, out_cols],
                        send_sem=out_send.at[target * 2 + cc], recv_sem=out_recv.at[me],
                        device_id={"row": target, "col": jnp.int32(cc)}, device_id_type=MESH,
                    )
                    copy.start() if act == "start" else copy.wait_send()

    for k in reversed(range(depth)):
        at = pick(z, [seq[k] for seq in order])
        rows = slab_of(at)
        for i in range(heads):
            scores = lax.dot_general(
                qn[i, rows, :], kn[i], (((1,), (1,)), ((), ())), preferred_element_type=jnp.float32
            )
            expo = jnp.exp(scores * (logit_scale[first_head + i] * inv_root))
            probs = (expo / jnp.sum(expo, axis=-1, keepdims=True)).astype(jnp.bfloat16)
            att[rows, i * head_dim:(i + 1) * head_dim] = jnp.dot(
                probs, vv[i], preferred_element_type=jnp.float32
            ).astype(jnp.bfloat16)
        out_copies(at, "start")

    for distance in range(depth):
        column(distance, "finish")
    for k in range(depth):
        part_copy(k).wait_send()
        cross_copy(k, pick(z, [seq[k] for seq in order])).wait_send()
    for at in range(depth):
        out_copies(at, "finish")
    for source in range(2 * row_count):

        @pl.when(source != me)
        def _():
            pltpu.make_async_remote_copy(
                src_ref=att.at[pl.ds(0, out_rows)], dst_ref=out.at[:, out_cols],
                send_sem=out_send.at[source], recv_sem=out_recv.at[source],
                device_id={"row": other_row}, device_id_type=MESH,
            ).wait_recv()


def fused(tokens, w_qkv, query_gain, key_gain, logit_scale):
    row_count = lax.axis_size("row")
    head_dim = query_gain.shape[0]
    local_heads = w_qkv.shape[1] // (3 * (head_dim // 2))
    heads = local_heads // 4
    span = w_qkv.shape[1] // 4
    tok_rows, width = tokens.shape
    count = tok_rows * row_count
    depth = row_count // FAST
    slab = FAST * tok_rows
    vmem, hbm = pl.BlockSpec(memory_space=pltpu.VMEM), pl.BlockSpec(memory_space=pl.ANY)
    dma = pltpu.SemaphoreType.DMA
    half = jnp.bfloat16
    return pl.pallas_call(
        functools.partial(fused_kernel, row_count, local_heads, head_dim),
        out_shape=jax.ShapeDtypeStruct((tok_rows // 2, row_count // 2 * local_heads * head_dim), half),
        in_specs=[hbm, hbm, vmem, vmem, pl.BlockSpec(memory_space=pltpu.SMEM)],
        out_specs=vmem,
        scratch_shapes=[
            pltpu.VMEM((count, width), half),
            pltpu.VMEM(w_qkv.shape, half),
            pltpu.VMEM((depth, slab, 2 * span), jnp.float32),
            pltpu.VMEM((depth, slab, 2 * span), jnp.float32),
            pltpu.VMEM((slab, 2 * span), jnp.float32),
            pltpu.VMEM((2, count, span), half),
            pltpu.VMEM((depth, slab, span), half),
            pltpu.VMEM((heads, count, head_dim), half),
            pltpu.VMEM((heads, count, head_dim), half),
            pltpu.VMEM((heads, count, head_dim), half),
            pltpu.VMEM((count, heads * head_dim), half),
            dma, dma((4,)), dma((3, row_count)), dma((row_count,)), dma((depth,)), dma((depth,)),
            dma((depth,)), dma((depth,)), dma((2 * row_count,)), dma((2 * row_count,)), dma,
        ],
        compiler_params=pltpu.CompilerParams(
            collective_id=0, has_side_effects=True, vmem_limit_bytes=60 * 2**20
        ),
        name="fused_attention",
    )(tokens, w_qkv, query_gain.reshape(1, -1), key_gain.reshape(1, -1), logit_scale)


def passed_along(block, axis, distance):
    devices = range(lax.axis_size(axis))
    route = [((i - distance) % len(devices), i) for i in devices]
    return lax.ppermute(block, axis, route)


def rms_scale(values, gain):
    wide = values.astype(jnp.float32)
    power = jnp.mean(wide * wide, axis=-1, keepdims=True)
    return (wide * lax.rsqrt(power + 1e-06) * gain).astype(jnp.bfloat16)


def body(tokens, w_qkv, query_gain, key_gain, logit_scale):
    row_count = lax.axis_size("row")
    half_rows = row_count // 2
    row_rank = lax.axis_index("row")
    side = row_rank // half_rows
    head_group = row_rank % half_rows
    head_dim = query_gain.shape[0]
    half_dim = head_dim // 2
    local_heads = w_qkv.shape[1] // (3 * half_dim)
    tok_rows = tokens.shape[0]
    quarter = tok_rows // 4
    terms = jnp.dot(
        lax.all_gather(tokens, "row", axis=0, tiled=True), w_qkv, preferred_element_type=jnp.float32
    )
    terms = terms.reshape(row_count, 2, tok_rows // 2, -1).transpose(1, 0, 2, 3)
    terms = terms.reshape(2, row_count * (tok_rows // 2), -1)
    mine = lax.psum_scatter(terms, "col", scatter_dimension=0, tiled=True)[0].astype(jnp.bfloat16)
    own_rows = mine.shape[0]
    other = passed_along(mine, "row", half_rows)
    leading = jnp.where(side == 0, mine, other).reshape(own_rows, local_heads, 3, half_dim)
    trailing = jnp.where(side == 0, other, mine).reshape(own_rows, local_heads, 3, half_dim)
    joined = jnp.concatenate([leading, trailing], axis=-1)
    query_normed = rms_scale(joined[:, :, 0], query_gain)
    key_normed = rms_scale(joined[:, :, 1], key_gain)
    keyval = jnp.stack([key_normed, joined[:, :, 2]], axis=2)
    keyval = lax.all_gather(keyval, "col", axis=0, tiled=True)
    key_all = keyval[:, :, 0]
    value_all = keyval[:, :, 1]
    split_queries = query_normed.reshape(row_count, 2, quarter, local_heads, head_dim)
    queries = jnp.where(side == 0, split_queries[:, 0], split_queries[:, 1])
    queries = queries.reshape(row_count * quarter, local_heads, head_dim)
    scales = lax.dynamic_slice_in_dim(logit_scale, head_group * local_heads, local_heads)
    inv_root = 1.0 / math.sqrt(head_dim)
    scores = jnp.einsum("qhd,khd->hqk", queries, key_all, preferred_element_type=jnp.float32)
    scores = scores * (scales * inv_root)[:, None, None]
    expo = jnp.exp(scores)
    probs = (expo / jnp.sum(expo, axis=-1, keepdims=True)).astype(jnp.bfloat16)
    mixed = jnp.einsum("hqk,khd->qhd", probs, value_all, preferred_element_type=jnp.float32).astype(
        jnp.bfloat16
    )
    mixed = mixed.reshape(row_count, quarter, local_heads * head_dim)
    landed = lax.all_to_all(mixed, "row", split_axis=0, concat_axis=0, tiled=True)
    landed = landed.reshape(2, half_rows, quarter, local_heads * head_dim).transpose(0, 2, 1, 3)
    return landed.reshape(2 * quarter, half_rows * local_heads * head_dim)


def fits(mesh, head_dim, columns):
    row_count = mesh.shape["row"]
    local_heads = columns // row_count // (3 * (head_dim // 2))
    span = columns // row_count // 4
    return (
        mesh.shape["col"] == 2
        and row_count % (2 * FAST) == 0
        and head_dim % 128 == 0
        and local_heads % 8 == 0
        and 2 * span % TILE == 0
    )


def solution(mesh):
    in_specs = (P(("groups", "row"), "col"), P("col", "row"), P(), P(), P())
    out_specs = P(("groups", "row", "col"), None)

    def run(tokens, w_qkv, query_gain, key_gain, logit_scale):
        inner = fused if fits(mesh, query_gain.shape[0], w_qkv.shape[1]) else body
        placed = jax.shard_map(inner, mesh=mesh, in_specs=in_specs, out_specs=out_specs, check_vma=False)
        return placed(tokens, w_qkv, query_gain, key_gain, logit_scale)

    return run
```

```python
import functools
import math

import jax
import jax.numpy as jnp
from jax import lax
from jax.experimental import pallas as pl
from jax.experimental.pallas import tpu as pltpu
from jax.sharding import PartitionSpec as P

MESH = pl.DeviceIdType.MESH
FAST = 2
TILE = 256
END_HOLD, MID_HOLD = 3, 4


def visit_order(depth):
    return [sorted(range(depth), key=lambda other: (abs(other - z), other)) for z in range(depth)]


def pick(index, values):
    chosen = jnp.int32(values[0])
    for i, value in enumerate(values[1:], 1):
        chosen = jnp.where(index == i, jnp.int32(value), chosen)
    return chosen


def fused_kernel(
    row_count, local_heads, head_dim,
    tokens, w_qkv, query_gain, key_gain, logit_scale, out,
    toks, weights, part_out, part_in, acc, joined, crossing, qn, kn, vv, att,
    own_sem, w_sem, gather_send, gather_recv, part_send, part_recv,
    cross_send, cross_recv, out_send, out_recv, self_sem,
):
    depth = row_count // FAST
    half_rows = row_count // 2
    half_dim = head_dim // 2
    heads = local_heads // 4
    span = heads * 3 * half_dim
    tok_rows = tokens.shape[0]
    out_rows = tok_rows // 2
    slab = FAST * out_rows
    order = visit_order(depth)

    row = lax.axis_index("row")
    col = lax.axis_index("col")
    z = row // FAST
    x = lax.rem(row, FAST)
    side = row // half_rows
    group = lax.rem(row, half_rows)
    other_col = 1 - col
    other_row = lax.rem(row + half_rows, row_count)
    across = z * FAST + (1 - x)
    me = row * 2 + col

    def w_copy(dest_col, far):
        dest_side = side if far == 0 else 1 - side
        mine = 0 if dest_col is other_col else 1
        start = pl.multiple_of((dest_side * 2 + dest_col) * span, 128)
        return pltpu.make_async_copy(
            w_qkv.at[:, pl.ds(start, span)],
            weights.at[:, pl.ds((mine * 2 + far) * span, span)],
            w_sem.at[mine * 2 + far],
        )

    w_copies = [w_copy(c, far) for c in (other_col, col) for far in (0, 1)]
    def chunk_at(at, xx, half):
        start = ((at * 2 + half) * FAST + xx) * out_rows
        return pl.ds(pl.multiple_of(start, out_rows), out_rows)

    def own_half(half):
        return tokens.at[pl.ds(half * out_rows, out_rows)]

    own_copies = [
        pltpu.make_async_copy(own_half(half), toks.at[chunk_at(z, x, half)], own_sem.at[half])
        for half in (0, 1)
    ]
    for copy in own_copies + w_copies:
        copy.start()

    barrier = pltpu.get_barrier_semaphore()
    for step in range(row_count):
        for c in (0, 1):
            if step == 0 and c == 0:
                continue
            peer = lax.rem(row + step, row_count)
            pl.semaphore_signal(
                barrier, inc=1,
                device_id={"row": peer, "col": col if c == 0 else other_col},
                device_id_type=MESH,
            )
    pl.semaphore_wait(barrier, 2 * row_count - 1)

    def gather_copy(at, xx, half, way, target, source=None):
        index = (at * FAST + xx) * 2 + half
        place = toks.at[chunk_at(at, xx, half)]
        return pltpu.make_async_remote_copy(
            src_ref=place if source is None else source,
            dst_ref=place,
            send_sem=gather_send.at[way, index],
            recv_sem=gather_recv.at[index],
            device_id={"row": target},
            device_id_type=MESH,
        )

    def column(distance, half, act):
        for sign in (0,) if distance == 0 else (-1, 1):
            at = z + sign * distance
            source = own_half(half) if distance == 0 else None

            @pl.when(jnp.logical_and(at >= 0, at < depth))
            def _():
                if act == "start" and distance:
                    gather_copy(at, x, half, 0, across).wait_recv()

                def go(copy):
                    if act == "start":
                        copy.start()
                    else:
                        copy.wait_send()

                if sign <= 0:

                    @pl.when(z + 1 < depth)
                    def _():
                        go(gather_copy(at, x, half, 1, row + FAST, source))

                if sign >= 0:

                    @pl.when(z >= 1)
                    def _():
                        go(gather_copy(at, x, half, 2, row - FAST, source))

                go(gather_copy(at, x, half, 0, across, source))

    def part_copy(step):
        return pltpu.make_async_remote_copy(
            src_ref=part_out.at[step], dst_ref=part_in.at[step],
            send_sem=part_send.at[step], recv_sem=part_recv.at[step],
            device_id={"col": other_col}, device_id_type=MESH,
        )

    def batch_at(step):
        return pick(z, [seq[step // 2] for seq in order]) * 2 + step % 2

    def slab_of(at):
        return pl.ds(pl.multiple_of(at * slab, slab), slab)

    def cross_copy(step, at):
        return pltpu.make_async_remote_copy(
            src_ref=crossing.at[step], dst_ref=joined.at[side, slab_of(at)],
            send_sem=cross_send.at[step], recv_sem=cross_recv.at[at],
            device_id={"row": other_row}, device_id_type=MESH,
        )

    def batch(step):
        at = batch_at(step)
        gather_copy(pick(z, [seq[step // 2] for seq in order]), 1 - x, step % 2, 0, across).wait_recv()
        if step < 2:
            own_copies[step].wait()
        if step == 0:
            for copy in w_copies:
                copy.wait()
        rows = slab_of(at)
        tiles = 2 * span // TILE

        @pl.loop(0, tiles)
        def _(n):
            part_out[step, :, pl.ds(pl.multiple_of(n * TILE, TILE), TILE)] = jnp.dot(
                toks[rows, :], weights[:, pl.ds(pl.multiple_of(n * TILE, TILE), TILE)],
                preferred_element_type=jnp.float32,
            )

        part_copy(step).start()

        @pl.loop(0, tiles)
        def _(n):
            acc[:, pl.ds(pl.multiple_of(n * TILE, TILE), TILE)] = jnp.dot(
                toks[rows, :], weights[:, pl.ds(pl.multiple_of(2 * span + n * TILE, TILE), TILE)],
                preferred_element_type=jnp.float32,
            )

        part_copy(step).wait_recv()
        crossing[step] = (acc[:, span:] + part_in[step, :, span:]).astype(jnp.bfloat16)
        for is_end, hold in ((True, END_HOLD), (False, MID_HOLD)):
            first = min(hold, batches - 1)
            ready = [step] if step > first else list(range(step + 1)) if step == first else []
            if ready:

                @pl.when(at_end if is_end else jnp.logical_not(at_end))
                def _():
                    for earlier in ready:
                        cross_copy(earlier, batch_at(earlier)).start()

        joined[side, rows, :] = (acc[:, :span] + part_in[step, :, :span]).astype(jnp.bfloat16)

    at_end = jnp.logical_or(z == 0, z == depth - 1)
    batches = 2 * depth
    column(0, 0, "start")
    column(0, 1, "start")
    column(1, 0, "start")
    for step in range(batches):
        batch(step)
        if step + 3 < batches:
            column((step + 3) // 2, (step + 3) % 2, "start")

    lanes = lax.broadcasted_iota(jnp.int32, (slab, head_dim), 1)
    low = lanes < half_dim

    def prepare(at):
        pltpu.make_async_remote_copy(
            src_ref=crossing.at[0], dst_ref=joined.at[1 - side, slab_of(at)],
            send_sem=cross_send.at[0], recv_sem=cross_recv.at[at],
            device_id={"row": other_row}, device_id_type=MESH,
        ).wait_recv()
        rows = slab_of(at)

        def pair(piece):
            first = joined[0, rows, piece * head_dim:(piece + 1) * head_dim].astype(jnp.float32)
            second = joined[1, rows, piece * head_dim:(piece + 1) * head_dim].astype(jnp.float32)
            return (
                jnp.where(low, first, pltpu.roll(second, half_dim, 1)),
                jnp.where(low, pltpu.roll(first, half_dim, 1), second),
            )

        def normed(wide, gain):
            power = jnp.mean(wide * wide, axis=-1, keepdims=True)
            return (wide * lax.rsqrt(power + 1e-06) * gain[...]).astype(jnp.bfloat16)

        for j in range(heads // 2):
            parts = [part for piece in range(3) for part in pair(3 * j + piece)]
            for i in range(2):
                query, key, value = parts[3 * i:3 * i + 3]
                qn[2 * j + i, rows, :] = normed(query, query_gain)
                kn[2 * j + i, rows, :] = normed(key, key_gain)
                vv[2 * j + i, rows, :] = value.astype(jnp.bfloat16)

    for step in range(batches):
        prepare(batch_at(step))

    first_head = group * local_heads + (side * 2 + col) * heads
    out_cols = pl.ds(pl.multiple_of(first_head * head_dim, heads * head_dim), heads * head_dim)
    inv_root = 1.0 / math.sqrt(head_dim)

    def out_copies(at, act):
        for xx in range(FAST):
            target = at // 2 * FAST + xx
            half = lax.rem(at, 2)
            source = att.at[chunk_at(at // 2, xx, half)]
            is_me = jnp.logical_and(target == row, col == half)

            @pl.when(is_me)
            def _():
                copy = pltpu.make_async_copy(source, out.at[:, out_cols], self_sem)
                copy.start() if act == "start" else copy.wait()

            @pl.when(jnp.logical_not(is_me))
            def _():
                copy = pltpu.make_async_remote_copy(
                    src_ref=source, dst_ref=out.at[:, out_cols],
                    send_sem=out_send.at[target * 2 + half], recv_sem=out_recv.at[me],
                    device_id={"row": target, "col": half}, device_id_type=MESH,
                )
                copy.start() if act == "start" else copy.wait_send()

    for k in reversed(range(depth)):
        at = pick(z, [seq[k] for seq in order])
        rows = pl.ds(pl.multiple_of(at * 2 * slab, 2 * slab), 2 * slab)
        for i in range(heads):
            scores = lax.dot_general(
                qn[i, rows, :], kn[i], (((1,), (1,)), ((), ())), preferred_element_type=jnp.float32
            )
            expo = jnp.exp(scores * (logit_scale[first_head + i] * inv_root))
            probs = (expo / jnp.sum(expo, axis=-1, keepdims=True)).astype(jnp.bfloat16)
            att[rows, i * head_dim:(i + 1) * head_dim] = jnp.dot(
                probs, vv[i], preferred_element_type=jnp.float32
            ).astype(jnp.bfloat16)
        out_copies(at * 2, "start")
        out_copies(at * 2 + 1, "start")

    for distance in range(depth):
        for half in (0, 1):
            column(distance, half, "finish")
    for step in range(batches):
        part_copy(step).wait_send()
        cross_copy(step, batch_at(step)).wait_send()
    for at in range(batches):
        out_copies(jnp.int32(at), "finish")
    for source in range(2 * row_count):

        @pl.when(source != me)
        def _():
            pltpu.make_async_remote_copy(
                src_ref=att.at[pl.ds(0, out_rows)], dst_ref=out.at[:, out_cols],
                send_sem=out_send.at[source], recv_sem=out_recv.at[source],
                device_id={"row": other_row}, device_id_type=MESH,
            ).wait_recv()


def fused(tokens, w_qkv, query_gain, key_gain, logit_scale):
    row_count = lax.axis_size("row")
    head_dim = query_gain.shape[0]
    local_heads = w_qkv.shape[1] // (3 * (head_dim // 2))
    heads = local_heads // 4
    span = w_qkv.shape[1] // 4
    tok_rows, width = tokens.shape
    count = tok_rows * row_count
    batches = row_count // FAST * 2
    slab = FAST * tok_rows // 2
    vmem, hbm = pl.BlockSpec(memory_space=pltpu.VMEM), pl.BlockSpec(memory_space=pl.ANY)
    dma = pltpu.SemaphoreType.DMA
    half = jnp.bfloat16
    return pl.pallas_call(
        functools.partial(fused_kernel, row_count, local_heads, head_dim),
        out_shape=jax.ShapeDtypeStruct((tok_rows // 2, row_count // 2 * local_heads * head_dim), half),
        in_specs=[hbm, hbm, vmem, vmem, pl.BlockSpec(memory_space=pltpu.SMEM)],
        out_specs=vmem,
        scratch_shapes=[
            pltpu.VMEM((count, width), half),
            pltpu.VMEM(w_qkv.shape, half),
            pltpu.VMEM((batches, slab, 2 * span), jnp.float32),
            pltpu.VMEM((batches, slab, 2 * span), jnp.float32),
            pltpu.VMEM((slab, 2 * span), jnp.float32),
            pltpu.VMEM((2, count, span), half),
            pltpu.VMEM((batches, slab, span), half),
            pltpu.VMEM((heads, count, head_dim), half),
            pltpu.VMEM((heads, count, head_dim), half),
            pltpu.VMEM((heads, count, head_dim), half),
            pltpu.VMEM((count, heads * head_dim), half),
            dma((2,)), dma((4,)), dma((3, 2 * row_count)), dma((2 * row_count,)), dma((batches,)),
            dma((batches,)), dma((batches,)), dma((batches,)), dma((2 * row_count,)), dma((2 * row_count,)), dma,
        ],
        compiler_params=pltpu.CompilerParams(
            collective_id=0, has_side_effects=True, vmem_limit_bytes=60 * 2**20
        ),
        name="fused_attention",
    )(tokens, w_qkv, query_gain.reshape(1, -1), key_gain.reshape(1, -1), logit_scale)


def passed_along(block, axis, distance):
    devices = range(lax.axis_size(axis))
    route = [((i - distance) % len(devices), i) for i in devices]
    return lax.ppermute(block, axis, route)


def rms_scale(values, gain):
    wide = values.astype(jnp.float32)
    power = jnp.mean(wide * wide, axis=-1, keepdims=True)
    return (wide * lax.rsqrt(power + 1e-06) * gain).astype(jnp.bfloat16)


def body(tokens, w_qkv, query_gain, key_gain, logit_scale):
    row_count = lax.axis_size("row")
    half_rows = row_count // 2
    row_rank = lax.axis_index("row")
    side = row_rank // half_rows
    head_group = row_rank % half_rows
    head_dim = query_gain.shape[0]
    half_dim = head_dim // 2
    local_heads = w_qkv.shape[1] // (3 * half_dim)
    tok_rows = tokens.shape[0]
    quarter = tok_rows // 4
    terms = jnp.dot(
        lax.all_gather(tokens, "row", axis=0, tiled=True), w_qkv, preferred_element_type=jnp.float32
    )
    terms = terms.reshape(row_count, 2, tok_rows // 2, -1).transpose(1, 0, 2, 3)
    terms = terms.reshape(2, row_count * (tok_rows // 2), -1)
    mine = lax.psum_scatter(terms, "col", scatter_dimension=0, tiled=True)[0].astype(jnp.bfloat16)
    own_rows = mine.shape[0]
    other = passed_along(mine, "row", half_rows)
    leading = jnp.where(side == 0, mine, other).reshape(own_rows, local_heads, 3, half_dim)
    trailing = jnp.where(side == 0, other, mine).reshape(own_rows, local_heads, 3, half_dim)
    joined = jnp.concatenate([leading, trailing], axis=-1)
    query_normed = rms_scale(joined[:, :, 0], query_gain)
    key_normed = rms_scale(joined[:, :, 1], key_gain)
    keyval = jnp.stack([key_normed, joined[:, :, 2]], axis=2)
    keyval = lax.all_gather(keyval, "col", axis=0, tiled=True)
    key_all = keyval[:, :, 0]
    value_all = keyval[:, :, 1]
    split_queries = query_normed.reshape(row_count, 2, quarter, local_heads, head_dim)
    queries = jnp.where(side == 0, split_queries[:, 0], split_queries[:, 1])
    queries = queries.reshape(row_count * quarter, local_heads, head_dim)
    scales = lax.dynamic_slice_in_dim(logit_scale, head_group * local_heads, local_heads)
    inv_root = 1.0 / math.sqrt(head_dim)
    scores = jnp.einsum("qhd,khd->hqk", queries, key_all, preferred_element_type=jnp.float32)
    scores = scores * (scales * inv_root)[:, None, None]
    expo = jnp.exp(scores)
    probs = (expo / jnp.sum(expo, axis=-1, keepdims=True)).astype(jnp.bfloat16)
    mixed = jnp.einsum("hqk,khd->qhd", probs, value_all, preferred_element_type=jnp.float32).astype(
        jnp.bfloat16
    )
    mixed = mixed.reshape(row_count, quarter, local_heads * head_dim)
    landed = lax.all_to_all(mixed, "row", split_axis=0, concat_axis=0, tiled=True)
    landed = landed.reshape(2, half_rows, quarter, local_heads * head_dim).transpose(0, 2, 1, 3)
    return landed.reshape(2 * quarter, half_rows * local_heads * head_dim)


def fits(mesh, head_dim, columns):
    row_count = mesh.shape["row"]
    local_heads = columns // row_count // (3 * (head_dim // 2))
    span = columns // row_count // 4
    return (
        mesh.shape["col"] == 2
        and row_count % (2 * FAST) == 0
        and head_dim % 128 == 0
        and local_heads % 8 == 0
        and 2 * span % TILE == 0
    )


def solution(mesh):
    in_specs = (P(("groups", "row"), "col"), P("col", "row"), P(), P(), P())
    out_specs = P(("groups", "row", "col"), None)

    def run(tokens, w_qkv, query_gain, key_gain, logit_scale):
        inner = fused if fits(mesh, query_gain.shape[0], w_qkv.shape[1]) else body
        placed = jax.shard_map(inner, mesh=mesh, in_specs=in_specs, out_specs=out_specs, check_vma=False)
        return placed(tokens, w_qkv, query_gain, key_gain, logit_scale)

    return run
```

```python
import functools
import math

import jax
import jax.numpy as jnp
from jax import lax
from jax.experimental import pallas as pl
from jax.experimental.pallas import tpu as pltpu
from jax.sharding import PartitionSpec as P

MESH = pl.DeviceIdType.MESH
FAST = 2
TILE = 256
END_HOLD, MID_HOLD = 3, 4


def visit_order(depth):
    return [sorted(range(depth), key=lambda other: (abs(other - z), other)) for z in range(depth)]


def pick(index, values):
    chosen = jnp.int32(values[0])
    for i, value in enumerate(values[1:], 1):
        chosen = jnp.where(index == i, jnp.int32(value), chosen)
    return chosen


def fused_kernel(
    row_count, local_heads, head_dim,
    tokens, w_qkv, query_gain, key_gain, logit_scale, out,
    toks, weights, part_out, part_in, acc, joined, crossing, qn, kn, vv, att,
    own_sem, w_sem, gather_send, gather_recv, part_send, part_recv,
    cross_send, cross_recv, out_send, out_recv, self_sem,
):
    depth = row_count // FAST
    half_rows = row_count // 2
    half_dim = head_dim // 2
    heads = local_heads // 4
    span = heads * 3 * half_dim
    tok_rows = tokens.shape[0]
    out_rows = tok_rows // 2
    slab = FAST * out_rows
    order = visit_order(depth)

    row = lax.axis_index("row")
    col = lax.axis_index("col")
    z = row // FAST
    x = lax.rem(row, FAST)
    side = row // half_rows
    group = lax.rem(row, half_rows)
    other_col = 1 - col
    other_row = lax.rem(row + half_rows, row_count)
    across = z * FAST + (1 - x)
    me = row * 2 + col

    def w_copy(dest_col, far):
        dest_side = side if far == 0 else 1 - side
        mine = 0 if dest_col is other_col else 1
        start = pl.multiple_of((dest_side * 2 + dest_col) * span, 128)
        return pltpu.make_async_copy(
            w_qkv.at[:, pl.ds(start, span)],
            weights.at[:, pl.ds((mine * 2 + far) * span, span)],
            w_sem.at[mine * 2 + far],
        )

    w_copies = [w_copy(c, far) for c in (other_col, col) for far in (0, 1)]
    def chunk_at(at, xx, half):
        start = ((at * 2 + half) * FAST + xx) * out_rows
        return pl.ds(pl.multiple_of(start, out_rows), out_rows)

    def own_half(half):
        return tokens.at[pl.ds(half * out_rows, out_rows)]

    own_copies = [
        pltpu.make_async_copy(own_half(half), toks.at[chunk_at(z, x, half)], own_sem.at[half])
        for half in (0, 1)
    ]
    for copy in own_copies + w_copies:
        copy.start()

    barrier = pltpu.get_barrier_semaphore()
    def greet(target):
        pl.semaphore_signal(barrier, inc=1, device_id=target, device_id_type=MESH)

    greet({"col": other_col})
    greet({"row": across})
    greet({"row": other_row})

    @pl.when(z + 1 < depth)
    def _():
        greet({"row": row + FAST})

    @pl.when(z >= 1)
    def _():
        greet({"row": row - FAST})

    below = jnp.where(z >= 1, jnp.int32(1), jnp.int32(0))
    above = jnp.where(z + 1 < depth, jnp.int32(1), jnp.int32(0))
    pl.semaphore_wait(barrier, 3 + below + above)

    def gather_copy(at, xx, half, way, target, source=None):
        index = (at * FAST + xx) * 2 + half
        place = toks.at[chunk_at(at, xx, half)]
        return pltpu.make_async_remote_copy(
            src_ref=place if source is None else source,
            dst_ref=place,
            send_sem=gather_send.at[way, index],
            recv_sem=gather_recv.at[index],
            device_id={"row": target},
            device_id_type=MESH,
        )

    def column(distance, half, act):
        for sign in (0,) if distance == 0 else (-1, 1):
            at = z + sign * distance
            source = own_half(half) if distance == 0 else None

            @pl.when(jnp.logical_and(at >= 0, at < depth))
            def _():
                if act == "start" and distance:
                    gather_copy(at, x, half, 0, across).wait_recv()

                def go(copy):
                    if act == "start":
                        copy.start()
                    else:
                        copy.wait_send()

                if sign <= 0:

                    @pl.when(z + 1 < depth)
                    def _():
                        go(gather_copy(at, x, half, 1, row + FAST, source))

                if sign >= 0:

                    @pl.when(z >= 1)
                    def _():
                        go(gather_copy(at, x, half, 2, row - FAST, source))

                go(gather_copy(at, x, half, 0, across, source))

    def part_copy(step):
        return pltpu.make_async_remote_copy(
            src_ref=part_out.at[step], dst_ref=part_in.at[step],
            send_sem=part_send.at[step], recv_sem=part_recv.at[step],
            device_id={"col": other_col}, device_id_type=MESH,
        )

    def batch_at(step):
        return pick(z, [seq[step // 2] for seq in order]) * 2 + step % 2

    def slab_of(at):
        return pl.ds(pl.multiple_of(at * slab, slab), slab)

    def cross_copy(step, at):
        return pltpu.make_async_remote_copy(
            src_ref=crossing.at[step], dst_ref=joined.at[side, slab_of(at)],
            send_sem=cross_send.at[step], recv_sem=cross_recv.at[at],
            device_id={"row": other_row}, device_id_type=MESH,
        )

    def batch(step):
        at = batch_at(step)
        gather_copy(pick(z, [seq[step // 2] for seq in order]), 1 - x, step % 2, 0, across).wait_recv()
        if step < 2:
            own_copies[step].wait()
        if step == 0:
            for copy in w_copies:
                copy.wait()
        rows = slab_of(at)
        tiles = 2 * span // TILE

        @pl.loop(0, tiles)
        def _(n):
            part_out[step, :, pl.ds(pl.multiple_of(n * TILE, TILE), TILE)] = jnp.dot(
                toks[rows, :], weights[:, pl.ds(pl.multiple_of(n * TILE, TILE), TILE)],
                preferred_element_type=jnp.float32,
            )

        part_copy(step).start()

        @pl.loop(0, tiles)
        def _(n):
            acc[:, pl.ds(pl.multiple_of(n * TILE, TILE), TILE)] = jnp.dot(
                toks[rows, :], weights[:, pl.ds(pl.multiple_of(2 * span + n * TILE, TILE), TILE)],
                preferred_element_type=jnp.float32,
            )

        part_copy(step).wait_recv()
        crossing[step] = (acc[:, span:] + part_in[step, :, span:]).astype(jnp.bfloat16)
        for is_end, hold in ((True, END_HOLD), (False, MID_HOLD)):
            first = min(hold, batches - 1)
            ready = [step] if step > first else list(range(step + 1)) if step == first else []
            if ready:

                @pl.when(at_end if is_end else jnp.logical_not(at_end))
                def _():
                    for earlier in ready:
                        cross_copy(earlier, batch_at(earlier)).start()

        joined[side, rows, :] = (acc[:, :span] + part_in[step, :, :span]).astype(jnp.bfloat16)

    at_end = jnp.logical_or(z == 0, z == depth - 1)
    batches = 2 * depth
    column(0, 0, "start")
    column(0, 1, "start")
    column(1, 0, "start")
    for step in range(batches):
        batch(step)
        if step + 3 < batches:
            column((step + 3) // 2, (step + 3) % 2, "start")

    lanes = lax.broadcasted_iota(jnp.int32, (slab, head_dim), 1)
    low = lanes < half_dim

    def prepare(at):
        pltpu.make_async_remote_copy(
            src_ref=crossing.at[0], dst_ref=joined.at[1 - side, slab_of(at)],
            send_sem=cross_send.at[0], recv_sem=cross_recv.at[at],
            device_id={"row": other_row}, device_id_type=MESH,
        ).wait_recv()
        rows = slab_of(at)

        def pair(piece):
            first = joined[0, rows, piece * head_dim:(piece + 1) * head_dim].astype(jnp.float32)
            second = joined[1, rows, piece * head_dim:(piece + 1) * head_dim].astype(jnp.float32)
            return (
                jnp.where(low, first, pltpu.roll(second, half_dim, 1)),
                jnp.where(low, pltpu.roll(first, half_dim, 1), second),
            )

        def normed(wide, gain):
            power = jnp.mean(wide * wide, axis=-1, keepdims=True)
            return (wide * lax.rsqrt(power + 1e-06) * gain[...]).astype(jnp.bfloat16)

        for j in range(heads // 2):
            parts = [part for piece in range(3) for part in pair(3 * j + piece)]
            for i in range(2):
                query, key, value = parts[3 * i:3 * i + 3]
                qn[2 * j + i, rows, :] = normed(query, query_gain)
                kn[2 * j + i, rows, :] = normed(key, key_gain)
                vv[2 * j + i, rows, :] = value.astype(jnp.bfloat16)

    for step in range(batches):
        prepare(batch_at(step))

    first_head = group * local_heads + (side * 2 + col) * heads
    out_cols = pl.ds(pl.multiple_of(first_head * head_dim, heads * head_dim), heads * head_dim)
    inv_root = 1.0 / math.sqrt(head_dim)

    def out_copies(at, act):
        for xx in range(FAST):
            target = at // 2 * FAST + xx
            half = lax.rem(at, 2)
            source = att.at[chunk_at(at // 2, xx, half)]
            is_me = jnp.logical_and(target == row, col == half)

            @pl.when(is_me)
            def _():
                copy = pltpu.make_async_copy(source, out.at[:, out_cols], self_sem)
                copy.start() if act == "start" else copy.wait()

            @pl.when(jnp.logical_not(is_me))
            def _():
                copy = pltpu.make_async_remote_copy(
                    src_ref=source, dst_ref=out.at[:, out_cols],
                    send_sem=out_send.at[target * 2 + half], recv_sem=out_recv.at[me],
                    device_id={"row": target, "col": half}, device_id_type=MESH,
                )
                copy.start() if act == "start" else copy.wait_send()

    for k in reversed(range(depth)):
        at = pick(z, [seq[k] for seq in order])
        rows = pl.ds(pl.multiple_of(at * 2 * slab, 2 * slab), 2 * slab)
        for i in range(heads):
            scores = lax.dot_general(
                qn[i, rows, :], kn[i], (((1,), (1,)), ((), ())), preferred_element_type=jnp.float32
            )
            expo = jnp.exp(scores * (logit_scale[first_head + i] * inv_root))
            probs = (expo / jnp.sum(expo, axis=-1, keepdims=True)).astype(jnp.bfloat16)
            att[rows, i * head_dim:(i + 1) * head_dim] = jnp.dot(
                probs, vv[i], preferred_element_type=jnp.float32
            ).astype(jnp.bfloat16)
        out_copies(at * 2, "start")
        out_copies(at * 2 + 1, "start")

    for distance in range(depth):
        for half in (0, 1):
            column(distance, half, "finish")
    for step in range(batches):
        part_copy(step).wait_send()
        cross_copy(step, batch_at(step)).wait_send()
    for at in range(batches):
        out_copies(jnp.int32(at), "finish")
    for source in range(2 * row_count):

        @pl.when(source != me)
        def _():
            pltpu.make_async_remote_copy(
                src_ref=att.at[pl.ds(0, out_rows)], dst_ref=out.at[:, out_cols],
                send_sem=out_send.at[source], recv_sem=out_recv.at[source],
                device_id={"row": other_row}, device_id_type=MESH,
            ).wait_recv()


def fused(tokens, w_qkv, query_gain, key_gain, logit_scale):
    row_count = lax.axis_size("row")
    head_dim = query_gain.shape[0]
    local_heads = w_qkv.shape[1] // (3 * (head_dim // 2))
    heads = local_heads // 4
    span = w_qkv.shape[1] // 4
    tok_rows, width = tokens.shape
    count = tok_rows * row_count
    batches = row_count // FAST * 2
    slab = FAST * tok_rows // 2
    vmem, hbm = pl.BlockSpec(memory_space=pltpu.VMEM), pl.BlockSpec(memory_space=pl.ANY)
    dma = pltpu.SemaphoreType.DMA
    half = jnp.bfloat16
    return pl.pallas_call(
        functools.partial(fused_kernel, row_count, local_heads, head_dim),
        out_shape=jax.ShapeDtypeStruct((tok_rows // 2, row_count // 2 * local_heads * head_dim), half),
        in_specs=[hbm, hbm, vmem, vmem, pl.BlockSpec(memory_space=pltpu.SMEM)],
        out_specs=vmem,
        scratch_shapes=[
            pltpu.VMEM((count, width), half),
            pltpu.VMEM(w_qkv.shape, half),
            pltpu.VMEM((batches, slab, 2 * span), jnp.float32),
            pltpu.VMEM((batches, slab, 2 * span), jnp.float32),
            pltpu.VMEM((slab, 2 * span), jnp.float32),
            pltpu.VMEM((2, count, span), half),
            pltpu.VMEM((batches, slab, span), half),
            pltpu.VMEM((heads, count, head_dim), half),
            pltpu.VMEM((heads, count, head_dim), half),
            pltpu.VMEM((heads, count, head_dim), half),
            pltpu.VMEM((count, heads * head_dim), half),
            dma((2,)), dma((4,)), dma((3, 2 * row_count)), dma((2 * row_count,)), dma((batches,)),
            dma((batches,)), dma((batches,)), dma((batches,)), dma((2 * row_count,)), dma((2 * row_count,)), dma,
        ],
        compiler_params=pltpu.CompilerParams(
            collective_id=0, has_side_effects=True, vmem_limit_bytes=60 * 2**20
        ),
        name="fused_attention",
    )(tokens, w_qkv, query_gain.reshape(1, -1), key_gain.reshape(1, -1), logit_scale)


def passed_along(block, axis, distance):
    devices = range(lax.axis_size(axis))
    route = [((i - distance) % len(devices), i) for i in devices]
    return lax.ppermute(block, axis, route)


def rms_scale(values, gain):
    wide = values.astype(jnp.float32)
    power = jnp.mean(wide * wide, axis=-1, keepdims=True)
    return (wide * lax.rsqrt(power + 1e-06) * gain).astype(jnp.bfloat16)


def body(tokens, w_qkv, query_gain, key_gain, logit_scale):
    row_count = lax.axis_size("row")
    half_rows = row_count // 2
    row_rank = lax.axis_index("row")
    side = row_rank // half_rows
    head_group = row_rank % half_rows
    head_dim = query_gain.shape[0]
    half_dim = head_dim // 2
    local_heads = w_qkv.shape[1] // (3 * half_dim)
    tok_rows = tokens.shape[0]
    quarter = tok_rows // 4
    terms = jnp.dot(
        lax.all_gather(tokens, "row", axis=0, tiled=True), w_qkv, preferred_element_type=jnp.float32
    )
    terms = terms.reshape(row_count, 2, tok_rows // 2, -1).transpose(1, 0, 2, 3)
    terms = terms.reshape(2, row_count * (tok_rows // 2), -1)
    mine = lax.psum_scatter(terms, "col", scatter_dimension=0, tiled=True)[0].astype(jnp.bfloat16)
    own_rows = mine.shape[0]
    other = passed_along(mine, "row", half_rows)
    leading = jnp.where(side == 0, mine, other).reshape(own_rows, local_heads, 3, half_dim)
    trailing = jnp.where(side == 0, other, mine).reshape(own_rows, local_heads, 3, half_dim)
    joined = jnp.concatenate([leading, trailing], axis=-1)
    query_normed = rms_scale(joined[:, :, 0], query_gain)
    key_normed = rms_scale(joined[:, :, 1], key_gain)
    keyval = jnp.stack([key_normed, joined[:, :, 2]], axis=2)
    keyval = lax.all_gather(keyval, "col", axis=0, tiled=True)
    key_all = keyval[:, :, 0]
    value_all = keyval[:, :, 1]
    split_queries = query_normed.reshape(row_count, 2, quarter, local_heads, head_dim)
    queries = jnp.where(side == 0, split_queries[:, 0], split_queries[:, 1])
    queries = queries.reshape(row_count * quarter, local_heads, head_dim)
    scales = lax.dynamic_slice_in_dim(logit_scale, head_group * local_heads, local_heads)
    inv_root = 1.0 / math.sqrt(head_dim)
    scores = jnp.einsum("qhd,khd->hqk", queries, key_all, preferred_element_type=jnp.float32)
    scores = scores * (scales * inv_root)[:, None, None]
    expo = jnp.exp(scores)
    probs = (expo / jnp.sum(expo, axis=-1, keepdims=True)).astype(jnp.bfloat16)
    mixed = jnp.einsum("hqk,khd->qhd", probs, value_all, preferred_element_type=jnp.float32).astype(
        jnp.bfloat16
    )
    mixed = mixed.reshape(row_count, quarter, local_heads * head_dim)
    landed = lax.all_to_all(mixed, "row", split_axis=0, concat_axis=0, tiled=True)
    landed = landed.reshape(2, half_rows, quarter, local_heads * head_dim).transpose(0, 2, 1, 3)
    return landed.reshape(2 * quarter, half_rows * local_heads * head_dim)


def fits(mesh, head_dim, columns):
    row_count = mesh.shape["row"]
    local_heads = columns // row_count // (3 * (head_dim // 2))
    span = columns // row_count // 4
    return (
        mesh.shape["col"] == 2
        and row_count % (2 * FAST) == 0
        and head_dim % 128 == 0
        and local_heads % 8 == 0
        and 2 * span % TILE == 0
    )


def solution(mesh):
    in_specs = (P(("groups", "row"), "col"), P("col", "row"), P(), P(), P())
    out_specs = P(("groups", "row", "col"), None)

    def run(tokens, w_qkv, query_gain, key_gain, logit_scale):
        inner = fused if fits(mesh, query_gain.shape[0], w_qkv.shape[1]) else body
        placed = jax.shard_map(inner, mesh=mesh, in_specs=in_specs, out_specs=out_specs, check_vma=False)
        return placed(tokens, w_qkv, query_gain, key_gain, logit_scale)

    return run
```

```python
import functools
import math

import jax
import jax.numpy as jnp
from jax import lax
from jax.experimental import pallas as pl
from jax.experimental.pallas import tpu as pltpu
from jax.sharding import PartitionSpec as P

MESH = pl.DeviceIdType.MESH
FAST = 2
TILE = 256
END_HOLD, MID_HOLD = 2, 3


def visit_order(depth):
    return [sorted(range(depth), key=lambda other: (abs(other - z), other)) for z in range(depth)]


def pick(index, values):
    chosen = jnp.int32(values[0])
    for i, value in enumerate(values[1:], 1):
        chosen = jnp.where(index == i, jnp.int32(value), chosen)
    return chosen


def fused_kernel(
    row_count, local_heads, head_dim,
    tokens, w_qkv, query_gain, key_gain, logit_scale, out,
    toks, weights, part_out, part_in, acc, joined, crossing, qn, kn, vv, att,
    own_sem, w_sem, gather_send, gather_recv, part_send, part_recv,
    cross_send, cross_recv, out_send, out_recv, self_sem,
):
    depth = row_count // FAST
    half_rows = row_count // 2
    half_dim = head_dim // 2
    heads = local_heads // 4
    span = heads * 3 * half_dim
    tok_rows = tokens.shape[0]
    out_rows = tok_rows // 2
    slab = FAST * out_rows
    order = visit_order(depth)

    row = lax.axis_index("row")
    col = lax.axis_index("col")
    z = row // FAST
    x = lax.rem(row, FAST)
    side = row // half_rows
    group = lax.rem(row, half_rows)
    other_col = 1 - col
    other_row = lax.rem(row + half_rows, row_count)
    across = z * FAST + (1 - x)
    me = row * 2 + col

    def w_copy(dest_col, far):
        dest_side = side if far == 0 else 1 - side
        mine = 0 if dest_col is other_col else 1
        start = pl.multiple_of((dest_side * 2 + dest_col) * span, 128)
        return pltpu.make_async_copy(
            w_qkv.at[:, pl.ds(start, span)],
            weights.at[:, pl.ds((mine * 2 + far) * span, span)],
            w_sem.at[mine * 2 + far],
        )

    w_copies = [w_copy(c, far) for c in (other_col, col) for far in (0, 1)]
    def chunk_at(at, xx, half):
        start = ((at * 2 + half) * FAST + xx) * out_rows
        return pl.ds(pl.multiple_of(start, out_rows), out_rows)

    def own_half(half):
        return tokens.at[pl.ds(half * out_rows, out_rows)]

    own_copies = [
        pltpu.make_async_copy(own_half(half), toks.at[chunk_at(z, x, half)], own_sem.at[half])
        for half in (0, 1)
    ]
    for copy in own_copies + w_copies:
        copy.start()

    barrier = pltpu.get_barrier_semaphore()
    def greet(target):
        pl.semaphore_signal(barrier, inc=1, device_id=target, device_id_type=MESH)

    greet({"col": other_col})
    greet({"row": across})
    greet({"row": other_row})

    @pl.when(z + 1 < depth)
    def _():
        greet({"row": row + FAST})

    @pl.when(z >= 1)
    def _():
        greet({"row": row - FAST})

    below = jnp.where(z >= 1, jnp.int32(1), jnp.int32(0))
    above = jnp.where(z + 1 < depth, jnp.int32(1), jnp.int32(0))
    pl.semaphore_wait(barrier, 3 + below + above)

    def gather_copy(at, xx, half, way, target, source=None):
        index = (at * FAST + xx) * 2 + half
        place = toks.at[chunk_at(at, xx, half)]
        return pltpu.make_async_remote_copy(
            src_ref=place if source is None else source,
            dst_ref=place,
            send_sem=gather_send.at[way, index],
            recv_sem=gather_recv.at[index],
            device_id={"row": target},
            device_id_type=MESH,
        )

    def column(distance, half, act):
        for sign in (0,) if distance == 0 else (-1, 1):
            at = z + sign * distance
            source = own_half(half) if distance == 0 else None

            @pl.when(jnp.logical_and(at >= 0, at < depth))
            def _():
                if act == "start" and distance:
                    gather_copy(at, x, half, 0, across).wait_recv()

                def go(copy):
                    if act == "start":
                        copy.start()
                    else:
                        copy.wait_send()

                if sign <= 0:

                    @pl.when(z + 1 < depth)
                    def _():
                        go(gather_copy(at, x, half, 1, row + FAST, source))

                if sign >= 0:

                    @pl.when(z >= 1)
                    def _():
                        go(gather_copy(at, x, half, 2, row - FAST, source))

                go(gather_copy(at, x, half, 0, across, source))

    def part_copy(step):
        return pltpu.make_async_remote_copy(
            src_ref=part_out.at[step], dst_ref=part_in.at[step],
            send_sem=part_send.at[step], recv_sem=part_recv.at[step],
            device_id={"col": other_col}, device_id_type=MESH,
        )

    def batch_at(step):
        return pick(z, [seq[step // 2] for seq in order]) * 2 + step % 2

    def slab_of(at):
        return pl.ds(pl.multiple_of(at * slab, slab), slab)

    def cross_copy(step, at):
        return pltpu.make_async_remote_copy(
            src_ref=crossing.at[step], dst_ref=joined.at[side, slab_of(at)],
            send_sem=cross_send.at[step], recv_sem=cross_recv.at[at],
            device_id={"row": other_row}, device_id_type=MESH,
        )

    def batch(step):
        at = batch_at(step)
        gather_copy(pick(z, [seq[step // 2] for seq in order]), 1 - x, step % 2, 0, across).wait_recv()
        if step < 2:
            own_copies[step].wait()
        if step == 0:
            for copy in w_copies:
                copy.wait()
        rows = slab_of(at)
        tiles = 2 * span // TILE

        @pl.loop(0, tiles)
        def _(n):
            part_out[step, :, pl.ds(pl.multiple_of(n * TILE, TILE), TILE)] = jnp.dot(
                toks[rows, :], weights[:, pl.ds(pl.multiple_of(n * TILE, TILE), TILE)],
                preferred_element_type=jnp.float32,
            ).astype(jnp.bfloat16)

        part_copy(step).start()

        @pl.loop(0, tiles)
        def _(n):
            acc[:, pl.ds(pl.multiple_of(n * TILE, TILE), TILE)] = jnp.dot(
                toks[rows, :], weights[:, pl.ds(pl.multiple_of(2 * span + n * TILE, TILE), TILE)],
                preferred_element_type=jnp.float32,
            )

        part_copy(step).wait_recv()
        crossing[step] = (acc[:, span:] + part_in[step, :, span:]).astype(jnp.bfloat16)
        for is_end, hold in ((True, END_HOLD), (False, MID_HOLD)):
            first = min(hold, batches - 1)
            ready = [step] if step > first else list(range(step + 1)) if step == first else []
            if ready:

                @pl.when(at_end if is_end else jnp.logical_not(at_end))
                def _():
                    for earlier in ready:
                        cross_copy(earlier, batch_at(earlier)).start()

        joined[side, rows, :] = (acc[:, :span] + part_in[step, :, :span]).astype(jnp.bfloat16)

    at_end = jnp.logical_or(z == 0, z == depth - 1)
    batches = 2 * depth
    column(0, 0, "start")
    column(0, 1, "start")
    column(1, 0, "start")
    for step in range(batches):
        batch(step)
        if step + 3 < batches:
            column((step + 3) // 2, (step + 3) % 2, "start")

    lanes = lax.broadcasted_iota(jnp.int32, (slab, head_dim), 1)
    low = lanes < half_dim

    def prepare(at):
        pltpu.make_async_remote_copy(
            src_ref=crossing.at[0], dst_ref=joined.at[1 - side, slab_of(at)],
            send_sem=cross_send.at[0], recv_sem=cross_recv.at[at],
            device_id={"row": other_row}, device_id_type=MESH,
        ).wait_recv()
        rows = slab_of(at)

        def pair(piece):
            first = joined[0, rows, piece * head_dim:(piece + 1) * head_dim].astype(jnp.float32)
            second = joined[1, rows, piece * head_dim:(piece + 1) * head_dim].astype(jnp.float32)
            return (
                jnp.where(low, first, pltpu.roll(second, half_dim, 1)),
                jnp.where(low, pltpu.roll(first, half_dim, 1), second),
            )

        def normed(wide, gain):
            power = jnp.mean(wide * wide, axis=-1, keepdims=True)
            return (wide * lax.rsqrt(power + 1e-06) * gain[...]).astype(jnp.bfloat16)

        for j in range(heads // 2):
            parts = [part for piece in range(3) for part in pair(3 * j + piece)]
            for i in range(2):
                query, key, value = parts[3 * i:3 * i + 3]
                qn[2 * j + i, rows, :] = normed(query, query_gain)
                kn[2 * j + i, rows, :] = normed(key, key_gain)
                vv[2 * j + i, rows, :] = value.astype(jnp.bfloat16)

    for step in range(batches):
        prepare(batch_at(step))

    first_head = group * local_heads + (side * 2 + col) * heads
    out_cols = pl.ds(pl.multiple_of(first_head * head_dim, heads * head_dim), heads * head_dim)
    inv_root = 1.0 / math.sqrt(head_dim)

    def out_copies(at, act):
        for xx in range(FAST):
            target = at // 2 * FAST + xx
            half = lax.rem(at, 2)
            source = att.at[chunk_at(at // 2, xx, half)]
            is_me = jnp.logical_and(target == row, col == half)

            @pl.when(is_me)
            def _():
                copy = pltpu.make_async_copy(source, out.at[:, out_cols], self_sem)
                copy.start() if act == "start" else copy.wait()

            @pl.when(jnp.logical_not(is_me))
            def _():
                copy = pltpu.make_async_remote_copy(
                    src_ref=source, dst_ref=out.at[:, out_cols],
                    send_sem=out_send.at[target * 2 + half], recv_sem=out_recv.at[me],
                    device_id={"row": target, "col": half}, device_id_type=MESH,
                )
                copy.start() if act == "start" else copy.wait_send()

    for k in reversed(range(depth)):
        at = pick(z, [seq[k] for seq in order])
        rows = pl.ds(pl.multiple_of(at * 2 * slab, 2 * slab), 2 * slab)
        for i in range(heads):
            scores = lax.dot_general(
                qn[i, rows, :], kn[i], (((1,), (1,)), ((), ())), preferred_element_type=jnp.float32
            )
            expo = jnp.exp(scores * (logit_scale[first_head + i] * inv_root))
            probs = (expo / jnp.sum(expo, axis=-1, keepdims=True)).astype(jnp.bfloat16)
            att[rows, i * head_dim:(i + 1) * head_dim] = jnp.dot(
                probs, vv[i], preferred_element_type=jnp.float32
            ).astype(jnp.bfloat16)
        out_copies(at * 2, "start")
        out_copies(at * 2 + 1, "start")

    for distance in range(depth):
        for half in (0, 1):
            column(distance, half, "finish")
    for step in range(batches):
        part_copy(step).wait_send()
        cross_copy(step, batch_at(step)).wait_send()
    for at in range(batches):
        out_copies(jnp.int32(at), "finish")
    for source in range(2 * row_count):

        @pl.when(source != me)
        def _():
            pltpu.make_async_remote_copy(
                src_ref=att.at[pl.ds(0, out_rows)], dst_ref=out.at[:, out_cols],
                send_sem=out_send.at[source], recv_sem=out_recv.at[source],
                device_id={"row": other_row}, device_id_type=MESH,
            ).wait_recv()


def fused(tokens, w_qkv, query_gain, key_gain, logit_scale):
    row_count = lax.axis_size("row")
    head_dim = query_gain.shape[0]
    local_heads = w_qkv.shape[1] // (3 * (head_dim // 2))
    heads = local_heads // 4
    span = w_qkv.shape[1] // 4
    tok_rows, width = tokens.shape
    count = tok_rows * row_count
    batches = row_count // FAST * 2
    slab = FAST * tok_rows // 2
    vmem, hbm = pl.BlockSpec(memory_space=pltpu.VMEM), pl.BlockSpec(memory_space=pl.ANY)
    dma = pltpu.SemaphoreType.DMA
    half = jnp.bfloat16
    return pl.pallas_call(
        functools.partial(fused_kernel, row_count, local_heads, head_dim),
        out_shape=jax.ShapeDtypeStruct((tok_rows // 2, row_count // 2 * local_heads * head_dim), half),
        in_specs=[hbm, hbm, vmem, vmem, pl.BlockSpec(memory_space=pltpu.SMEM)],
        out_specs=vmem,
        scratch_shapes=[
            pltpu.VMEM((count, width), half),
            pltpu.VMEM(w_qkv.shape, half),
            pltpu.VMEM((batches, slab, 2 * span), half),
            pltpu.VMEM((batches, slab, 2 * span), half),
            pltpu.VMEM((slab, 2 * span), jnp.float32),
            pltpu.VMEM((2, count, span), half),
            pltpu.VMEM((batches, slab, span), half),
            pltpu.VMEM((heads, count, head_dim), half),
            pltpu.VMEM((heads, count, head_dim), half),
            pltpu.VMEM((heads, count, head_dim), half),
            pltpu.VMEM((count, heads * head_dim), half),
            dma((2,)), dma((4,)), dma((3, 2 * row_count)), dma((2 * row_count,)), dma((batches,)),
            dma((batches,)), dma((batches,)), dma((batches,)), dma((2 * row_count,)), dma((2 * row_count,)), dma,
        ],
        compiler_params=pltpu.CompilerParams(
            collective_id=0, has_side_effects=True, vmem_limit_bytes=60 * 2**20
        ),
        name="fused_attention",
    )(tokens, w_qkv, query_gain.reshape(1, -1), key_gain.reshape(1, -1), logit_scale)


def passed_along(block, axis, distance):
    devices = range(lax.axis_size(axis))
    route = [((i - distance) % len(devices), i) for i in devices]
    return lax.ppermute(block, axis, route)


def rms_scale(values, gain):
    wide = values.astype(jnp.float32)
    power = jnp.mean(wide * wide, axis=-1, keepdims=True)
    return (wide * lax.rsqrt(power + 1e-06) * gain).astype(jnp.bfloat16)


def body(tokens, w_qkv, query_gain, key_gain, logit_scale):
    row_count = lax.axis_size("row")
    half_rows = row_count // 2
    row_rank = lax.axis_index("row")
    side = row_rank // half_rows
    head_group = row_rank % half_rows
    head_dim = query_gain.shape[0]
    half_dim = head_dim // 2
    local_heads = w_qkv.shape[1] // (3 * half_dim)
    tok_rows = tokens.shape[0]
    quarter = tok_rows // 4
    terms = jnp.dot(
        lax.all_gather(tokens, "row", axis=0, tiled=True), w_qkv, preferred_element_type=jnp.float32
    )
    terms = terms.reshape(row_count, 2, tok_rows // 2, -1).transpose(1, 0, 2, 3)
    terms = terms.reshape(2, row_count * (tok_rows // 2), -1)
    mine = lax.psum_scatter(terms, "col", scatter_dimension=0, tiled=True)[0].astype(jnp.bfloat16)
    own_rows = mine.shape[0]
    other = passed_along(mine, "row", half_rows)
    leading = jnp.where(side == 0, mine, other).reshape(own_rows, local_heads, 3, half_dim)
    trailing = jnp.where(side == 0, other, mine).reshape(own_rows, local_heads, 3, half_dim)
    joined = jnp.concatenate([leading, trailing], axis=-1)
    query_normed = rms_scale(joined[:, :, 0], query_gain)
    key_normed = rms_scale(joined[:, :, 1], key_gain)
    keyval = jnp.stack([key_normed, joined[:, :, 2]], axis=2)
    keyval = lax.all_gather(keyval, "col", axis=0, tiled=True)
    key_all = keyval[:, :, 0]
    value_all = keyval[:, :, 1]
    split_queries = query_normed.reshape(row_count, 2, quarter, local_heads, head_dim)
    queries = jnp.where(side == 0, split_queries[:, 0], split_queries[:, 1])
    queries = queries.reshape(row_count * quarter, local_heads, head_dim)
    scales = lax.dynamic_slice_in_dim(logit_scale, head_group * local_heads, local_heads)
    inv_root = 1.0 / math.sqrt(head_dim)
    scores = jnp.einsum("qhd,khd->hqk", queries, key_all, preferred_element_type=jnp.float32)
    scores = scores * (scales * inv_root)[:, None, None]
    expo = jnp.exp(scores)
    probs = (expo / jnp.sum(expo, axis=-1, keepdims=True)).astype(jnp.bfloat16)
    mixed = jnp.einsum("hqk,khd->qhd", probs, value_all, preferred_element_type=jnp.float32).astype(
        jnp.bfloat16
    )
    mixed = mixed.reshape(row_count, quarter, local_heads * head_dim)
    landed = lax.all_to_all(mixed, "row", split_axis=0, concat_axis=0, tiled=True)
    landed = landed.reshape(2, half_rows, quarter, local_heads * head_dim).transpose(0, 2, 1, 3)
    return landed.reshape(2 * quarter, half_rows * local_heads * head_dim)


def fits(mesh, head_dim, columns):
    row_count = mesh.shape["row"]
    local_heads = columns // row_count // (3 * (head_dim // 2))
    span = columns // row_count // 4
    return (
        mesh.shape["col"] == 2
        and row_count % (2 * FAST) == 0
        and head_dim % 128 == 0
        and local_heads % 8 == 0
        and 2 * span % TILE == 0
    )


def solution(mesh):
    in_specs = (P(("groups", "row"), "col"), P("col", "row"), P(), P(), P())
    out_specs = P(("groups", "row", "col"), None)

    def run(tokens, w_qkv, query_gain, key_gain, logit_scale):
        inner = fused if fits(mesh, query_gain.shape[0], w_qkv.shape[1]) else body
        placed = jax.shard_map(inner, mesh=mesh, in_specs=in_specs, out_specs=out_specs, check_vma=False)
        return placed(tokens, w_qkv, query_gain, key_gain, logit_scale)

    return run
```
